32 devices in a mesh: row: 8 (over y, x, core), col: 4 (over z).
Axes of the slice: x: 2, y: 2, z: 4, core: 2. Of those that a mesh axis runs over, the one named last changes fastest.
Arguments:
- integrals: bfloat16 [3072, 192], P('row', 'col'), may hold values from -0.4375 to 0.4375
- amplitudes: bfloat16 [192, 3072], P('row', 'col'), may hold values from -6 to 6
- energies: float32 [3072], replicated, may hold values from 0.5 to 4
Outputs:
- residual: float32 [3072, 3072], P('row', 'col')
The draws below stay inside these ranges and needn't reach their ends.
All inputs are finite; a program needn't handle non-finite values.
Results may differ from the reference program's by a relative error of at most 0.0021.
Values may be sent and summed in bfloat16 or wider, within the bound.
No kernel may reach another device: no remote copies, remote signals or barrier semaphores. Data moves between devices by JAX's collectives and lax.ppermute only.
A program may use at most 128 MiB of HBM per device.

```python
import math
import jax
import jax.numpy as jnp

NPAIR = 3072
KPAIR = 192


def steps_of(own_key, dims, pieces, smallest, high):
    def one(position, blocks):
        steps = jax.random.uniform(jax.random.fold_in(jax.random.fold_in(own_key, 6), position), (blocks,), jnp.float32, smallest / len(pieces), high / len(pieces))
        return jnp.repeat(jnp.exp(steps), dims[position] // blocks).reshape((-1,) + (1,) * (len(dims) - position - 1))

    loudness = one(*pieces[0])
    for cut in pieces[1:]:
        loudness = loudness * one(*cut)
    return loudness


def scatter_about(key, dims, width, bound, split=(), dtype=jnp.bfloat16):
    loudness = steps_of(key, dims, split, -0.22, 0.18) if split else 1.0
    values = jax.random.normal(key, dims, jnp.float32) * width * loudness
    return jnp.minimum(jnp.maximum(values, -bound), bound).astype(dtype)


def setup_inputs(seed: int = 0) -> dict:
    splits = jax.random.split(jax.random.key(seed), 4)
    return {
        "integrals": scatter_about(splits[0], (NPAIR, KPAIR), KPAIR ** -0.5, 0.4375, ((0, 8), (1, 4))),
        "amplitudes": scatter_about(splits[1], (KPAIR, NPAIR), 1.0, 6.0, ((0, 8), (1, 4))),
        "energies": jnp.clip(jnp.exp(jax.random.uniform(splits[2], (NPAIR,), jnp.float32, math.log(0.5), math.log(4.0))), 0.5, 4.0),
    }


def reference(integrals, amplitudes, energies):
    ladder = jnp.dot(integrals, amplitudes, preferred_element_type=jnp.float32)
    ladder_half = ladder.astype(jnp.bfloat16)
    denom = energies[:, None] + energies[None, :]
    return (ladder + ladder_half.T.astype(jnp.float32)) / denom
```

```python
import functools

import jax
import jax.numpy as jnp
from jax import lax
from jax.experimental import pallas as pl
from jax.experimental.pallas import tpu as pltpu
from jax.sharding import PartitionSpec as P

AXES = ("row", "col")
TILE = 128


def pick(index, pieces):
    return functools.reduce(
        lambda kept, i: jnp.where(index == i, pieces[i], kept),
        range(1, len(pieces)),
        pieces[0],
    )


def finish(n, kp, rt, *refs):
    gathered, settled = refs[:n], refs[n : 2 * n]
    swap_a, swap_b, energy, out, lhs, rhs, mir_l, mir_r, buffer, done = refs[2 * n :]
    row, col = lax.axis_index("row"), lax.axis_index("col")
    chip, core = row // 2, row % 2
    shift = chip ^ col

    @pl.when(core == 0)
    def _():
        for j in range(n):
            own = pl.ds(pl.multiple_of((shift ^ j) * kp, kp), kp)
            here = pl.ds(j * kp, kp)
            base = 2 * kp * j
            lhs[own, :] = gathered[j][:kp, :]
            rhs[here, :rt] = swap_a[base : base + kp, :]
            rhs[here, rt:] = swap_a[base + kp : base + 2 * kp, :]
            mir_l[here, :] = settled[j][:kp, :]
            mir_r[own, :rt] = swap_b[base : base + kp, :]
            mir_r[own, rt:] = swap_b[base + kp : base + 2 * kp, :]

    @pl.when(core == 1)
    def _():
        for j in range(n):
            own = pl.ds(pl.multiple_of((shift ^ j) * kp, kp), kp)
            here = pl.ds(j * kp, kp)
            base = 2 * kp * j
            lhs[own, :] = swap_a[base + kp : base + 2 * kp, :]
            rhs[here, :rt] = gathered[j][2 * kp : 3 * kp, :]
            rhs[here, rt:] = gathered[j][3 * kp :, :]
            mir_l[here, :] = swap_b[base + kp : base + 2 * kp, :]
            mir_r[own, :rt] = settled[j][:kp, :]
            mir_r[own, rt:] = settled[j][kp:, :]

    over_first = (((0,), (0,)), ((), ()))
    across = energy[:, pl.ds(pl.multiple_of(col * 2 * rt, 2 * rt), 2 * rt)]
    copies = []
    for i in range(rt // TILE):
        rows = slice(i * TILE, (i + 1) * TILE)
        ladder = lax.dot_general(
            lhs[:, rows], rhs[...], over_first, preferred_element_type=jnp.float32
        )
        partner = lax.dot_general(
            mir_l[:, rows], mir_r[...], over_first, preferred_element_type=jnp.float32
        )
        partner = partner.astype(jnp.bfloat16).astype(jnp.float32)
        along = energy[:, pl.ds(pl.multiple_of(row * rt + i * TILE, TILE), TILE)]
        down = jnp.broadcast_to(along, (TILE, TILE)).T[:, :1]
        buffer[rows, :] = (ladder + partner) / (down + across)
        copies.append(pltpu.make_async_copy(buffer.at[rows], out.at[rows], done.at[i]))
        copies[-1].start()
    for copy in copies:
        copy.wait()


def paired(integrals, amplitudes, energies):
    n = lax.axis_size("col")
    rt, kp = integrals.shape
    ka = amplitudes.shape[0]
    row, col = lax.axis_index("row"), lax.axis_index("col")
    chip, core = row // 2, row % 2
    shift = chip ^ col
    first = core == 0

    def send(value, target):
        pairs = [
            ((2 * k + h) * n + c, (2 * tk + th) * n + tc)
            for k in range(n)
            for h in range(2)
            for c in range(n)
            for tk, th, tc in [target(k, h, c)]
        ]
        return lax.ppermute(value, AXES, pairs)

    def other(k, h, c):
        return k, 1 - h, c

    own = jnp.concatenate([integrals.T, amplitudes[:, :rt], amplitudes[:, rt:]])
    own = lax.optimization_barrier(own)
    theirs = send(own, other)
    block = jnp.concatenate(
        [
            jnp.where(first, x[low:high], y[low:high])
            for low, high in ((0, kp), (kp, kp + ka), (kp + ka, kp + 2 * ka))
            for x, y in ((own, theirs), (theirs, own))
        ]
    )
    order = sorted(range(1, n), key=lambda j: bin(j).count("1"))
    gathered = {0: block}
    for j in order:
        gathered[j] = send(block, lambda k, h, c: (k ^ j * h, h, c ^ j * (1 - h)))
    gathered = [gathered[j] for j in range(n)]
    onward = [jnp.where(first, g[2 * kp :], g[: 2 * kp]) for g in gathered]
    settled = {0: pick(shift, onward)}
    for j in order:
        settled[j] = send(
            pick(shift ^ j, onward), lambda k, h, c: (k ^ j * (1 - h), h, c ^ j * h)
        )
    settled = [settled[j] for j in range(n)]
    swap_a = send(
        jnp.concatenate([jnp.where(first, g[: 2 * kp], g[2 * kp :]) for g in gathered]), other
    )
    swap_b = send(jnp.concatenate(settled), other)
    keep = pl.BlockSpec(memory_space=pltpu.VMEM)
    inputs = [*gathered, *settled, swap_a, swap_b, energies.reshape(1, -1)]
    return pl.pallas_call(
        functools.partial(finish, n, kp, rt),
        in_specs=[keep] * len(inputs),
        out_specs=pl.BlockSpec(memory_space=pl.ANY),
        out_shape=jax.ShapeDtypeStruct((rt, 2 * rt), jnp.float32),
        scratch_shapes=[
            *[pltpu.VMEM((n * kp, width), jnp.bfloat16) for width in (rt, 2 * rt, rt, 2 * rt)],
            pltpu.VMEM((rt, 2 * rt), jnp.float32),
            pltpu.SemaphoreType.DMA((rt // TILE,)),
        ],
        name="finish",
    )(*[pltpu.with_memory_space_constraint(x, pltpu.VMEM) for x in inputs])


def general(integrals, amplitudes, energies):
    rows_tile = integrals.shape[0]
    cols_tile = amplitudes.shape[1]
    n_row = lax.axis_size("row")
    n_col = lax.axis_size("col")
    block = rows_tile // n_col
    panel = lax.all_gather(integrals, "col", axis=1, tiled=True)
    ladder = jnp.dot(
        panel,
        lax.all_gather(amplitudes, "row", axis=0, tiled=True),
        preferred_element_type=jnp.float32,
    )
    rounded = ladder.astype(jnp.bfloat16)
    by_rows = lax.all_to_all(rounded, "col", split_axis=0, concat_axis=1, tiled=True)
    lifted = lax.all_to_all(by_rows, "row", split_axis=1, concat_axis=0, tiled=True)
    shaped = lifted.reshape(n_row, 1, block, n_col * block)
    settled = lax.all_to_all(shaped, "col", split_axis=0, concat_axis=1, tiled=True)
    partner = settled.reshape(n_row * block, n_col * block).T.astype(jnp.float32)
    row_start = lax.axis_index("row") * rows_tile
    col_start = lax.axis_index("col") * cols_tile
    row_energy = lax.dynamic_slice_in_dim(energies, row_start, rows_tile, 0)
    col_energy = lax.dynamic_slice_in_dim(energies, col_start, cols_tile, 0)
    return (ladder + partner) / (row_energy[:, None] + col_energy[None, :])


def body(integrals, amplitudes, energies):
    rt, kp = integrals.shape
    n_row, n_col = lax.axis_size("row"), lax.axis_size("col")
    fits = (
        n_row == 2 * n_col
        and n_col & (n_col - 1) == 0
        and amplitudes.shape == (kp // 2, 2 * rt)
        and rt % 128 == 0
        and kp % 16 == 0
    )
    return (paired if fits else general)(integrals, amplitudes, energies)


def solution(mesh):
    placed = (P("row", "col"), P("row", "col"), P())
    return jax.shard_map(
        body, mesh=mesh, in_specs=placed, out_specs=P("row", "col"), check_vma=False
    )
```

```python
import functools

import jax
import jax.numpy as jnp
from jax import lax
from jax.experimental import pallas as pl
from jax.experimental.pallas import tpu as pltpu
from jax.sharding import PartitionSpec as P

AXES = ("row", "col")
TILE = 128


def pick(index, pieces):
    return functools.reduce(
        lambda kept, i: jnp.where(index == i, pieces[i], kept),
        range(1, len(pieces)),
        pieces[0],
    )


def finish(n, kp, rt, *refs):
    direct, settled = refs[: n - 1], refs[n - 1 : 2 * n - 2]
    swap_d, swap_s, own_i, own_a, near_i, near_a, energy, out = refs[2 * n - 2 : 2 * n + 6]
    lhs, rhs, mir_l, mir_r, buffer, done = refs[2 * n + 6 :]
    row, col = lax.axis_index("row"), lax.axis_index("col")
    chip, core = row // 2, row % 2
    shift = chip ^ col

    def put(j, i_half, a_lo, a_hi, a_half, i_lo, i_hi):
        here = pl.ds(j * kp, kp)
        moved = pl.ds(pl.multiple_of((shift ^ j) * kp, kp), kp)
        lhs[moved, :] = i_half
        rhs[here, :rt] = a_lo
        rhs[here, rt:] = a_hi
        mir_l[here, :] = a_half
        mir_r[moved, :rt] = i_lo
        mir_r[moved, rt:] = i_hi

    for h in range(2):

        @pl.when(core == h)
        def _():
            def part(ref, i):
                return ref[i * kp : (i + 1) * kp, :]

            put(
                0,
                part(own_i, h),
                part(own_a, 0),
                part(own_a, 1),
                part(near_a, h),
                part(near_i, 0),
                part(near_i, 1),
            )
            for j in range(1, n):
                mine = [part(x[j - 1], i) for x in (direct, settled) for i in range(2)]
                gift = [part(x, 2 * (j - 1) + i) for x in (swap_d, swap_s) for i in range(2)]
                if h == 0:
                    put(j, gift[0], mine[0], mine[1], mine[2], gift[2], gift[3])
                else:
                    put(j, mine[1], gift[0], gift[1], gift[3], mine[2], mine[3])

    over_first = (((0,), (0,)), ((), ()))
    across = energy[:, pl.ds(pl.multiple_of(col * 2 * rt, 2 * rt), 2 * rt)]
    copies = []
    for i in range(rt // TILE):
        rows = slice(i * TILE, (i + 1) * TILE)
        ladder = lax.dot_general(
            lhs[:, rows], rhs[...], over_first, preferred_element_type=jnp.float32
        )
        partner = lax.dot_general(
            mir_l[:, rows], mir_r[...], over_first, preferred_element_type=jnp.float32
        )
        partner = partner.astype(jnp.bfloat16).astype(jnp.float32)
        along = energy[:, pl.ds(pl.multiple_of(row * rt + i * TILE, TILE), TILE)]
        down = jnp.broadcast_to(along, (TILE, TILE)).T[:, :1]
        buffer[rows, :] = (ladder + partner) / (down + across)
        copies.append(pltpu.make_async_copy(buffer.at[rows], out.at[rows], done.at[i]))
        copies[-1].start()
    for copy in copies:
        copy.wait()


def paired(integrals, amplitudes, energies):
    n = lax.axis_size("col")
    rt, kp = integrals.shape
    ka = amplitudes.shape[0]
    row, col = lax.axis_index("row"), lax.axis_index("col")
    chip, core = row // 2, row % 2
    shift = chip ^ col
    first = core == 0

    def send(value, target):
        pairs = [
            ((2 * k + h) * n + c, (2 * tk + th) * n + tc)
            for k in range(n)
            for h in range(2)
            for c in range(n)
            for tk, th, tc in [target(k, h, c)]
        ]
        return lax.ppermute(value, AXES, pairs)

    def other(k, h, c):
        return k, 1 - h, c

    def carrier(j):
        return 1 - j % 2

    their_i, their_a = send(integrals.T, other), send(amplitudes, other)
    mine = lax.optimization_barrier(
        jnp.concatenate([integrals.T, amplitudes[:, :rt], amplitudes[:, rt:]])
    )
    pairs = [
        (mine[:kp], their_i),
        (mine[kp : kp + ka], their_a[:, :rt]),
        (mine[kp + ka :], their_a[:, rt:]),
    ]
    packs = [(jnp.where(first, x, y), jnp.where(first, y, x)) for x, y in pairs]
    own_i = jnp.concatenate(packs[0])
    own_a = jnp.concatenate(packs[1] + packs[2])
    own = {h: jnp.where(core == h, own_a, own_i) for h in range(2)}
    order = range(n - 1, 0, -1)
    gathered, direct, settled = {0: own[carrier(0)]}, {}, {}
    for j in order:
        gathered[j] = send(
            own[carrier(j)],
            lambda k, h, c: (k, h, c ^ j) if h == carrier(j) else (k ^ j, h, c),
        )
    for j in order:
        direct[j] = send(
            own[carrier(j)],
            lambda k, h, c: (k ^ j, 0, c) if h == carrier(j) else (k, 1, c ^ j),
        )
    for j in order:
        settled[j] = send(
            pick(shift ^ j, gathered),
            lambda k, h, c: (k ^ j, 0, c) if h == carrier(k ^ c ^ j) else (k, 1, c ^ j),
        )
    near = pick(shift, gathered)
    far = send(near, other)
    has_a = functools.reduce(
        lambda kept, m: jnp.where(shift == m, core == carrier(m), kept), range(n), first
    )
    near_a, near_i = jnp.where(has_a, near, far), jnp.where(has_a, far, near)
    direct, settled = [[x[j] for j in range(1, n)] for x in (direct, settled)]
    swap_d, swap_s = send(jnp.concatenate(direct), other), send(jnp.concatenate(settled), other)
    keep = pl.BlockSpec(memory_space=pltpu.VMEM)
    inputs = [
        *direct,
        *settled,
        *[swap_d, swap_s, own_i, own_a, near_i, near_a, energies.reshape(1, -1)],
    ]
    return pl.pallas_call(
        functools.partial(finish, n, kp, rt),
        in_specs=[keep] * len(inputs),
        out_specs=pl.BlockSpec(memory_space=pl.ANY),
        out_shape=jax.ShapeDtypeStruct((rt, 2 * rt), jnp.float32),
        scratch_shapes=[
            *[pltpu.VMEM((n * kp, width), jnp.bfloat16) for width in (rt, 2 * rt, rt, 2 * rt)],
            pltpu.VMEM((rt, 2 * rt), jnp.float32),
            pltpu.SemaphoreType.DMA((rt // TILE,)),
        ],
        name="finish",
    )(*[pltpu.with_memory_space_constraint(x, pltpu.VMEM) for x in inputs])


def general(integrals, amplitudes, energies):
    rows_tile = integrals.shape[0]
    cols_tile = amplitudes.shape[1]
    n_row = lax.axis_size("row")
    n_col = lax.axis_size("col")
    block = rows_tile // n_col
    panel = lax.all_gather(integrals, "col", axis=1, tiled=True)
    ladder = jnp.dot(
        panel,
        lax.all_gather(amplitudes, "row", axis=0, tiled=True),
        preferred_element_type=jnp.float32,
    )
    rounded = ladder.astype(jnp.bfloat16)
    by_rows = lax.all_to_all(rounded, "col", split_axis=0, concat_axis=1, tiled=True)
    lifted = lax.all_to_all(by_rows, "row", split_axis=1, concat_axis=0, tiled=True)
    shaped = lifted.reshape(n_row, 1, block, n_col * block)
    settled = lax.all_to_all(shaped, "col", split_axis=0, concat_axis=1, tiled=True)
    partner = settled.reshape(n_row * block, n_col * block).T.astype(jnp.float32)
    row_start = lax.axis_index("row") * rows_tile
    col_start = lax.axis_index("col") * cols_tile
    row_energy = lax.dynamic_slice_in_dim(energies, row_start, rows_tile, 0)
    col_energy = lax.dynamic_slice_in_dim(energies, col_start, cols_tile, 0)
    return (ladder + partner) / (row_energy[:, None] + col_energy[None, :])


def body(integrals, amplitudes, energies):
    rt, kp = integrals.shape
    n_row, n_col = lax.axis_size("row"), lax.axis_size("col")
    fits = (
        n_row == 2 * n_col
        and n_col & (n_col - 1) == 0
        and amplitudes.shape == (kp // 2, 2 * rt)
        and rt % 128 == 0
        and kp % 16 == 0
    )
    return (paired if fits else general)(integrals, amplitudes, energies)


def solution(mesh):
    placed = (P("row", "col"), P("row", "col"), P())
    return jax.shard_map(
        body, mesh=mesh, in_specs=placed, out_specs=P("row", "col"), check_vma=False
    )
```

```python
import functools

import jax
import jax.numpy as jnp
from jax import lax
from jax.experimental import pallas as pl
from jax.experimental.pallas import tpu as pltpu
from jax.sharding import PartitionSpec as P


AXES = ("row", "col")
TILE = 128
SPLIT = 2
VMEM_LIMIT = 12 * 2**20
OVER_FIRST = (((0,), (0,)), ((), ()))


def pick(index, pieces):
    return functools.reduce(
        lambda kept, i: jnp.where(index == i, pieces[i], kept),
        range(1, len(pieces)),
        pieces[0],
    )


def place():
    row, col = lax.axis_index("row"), lax.axis_index("col")
    return row // 2, row % 2, (row // 2) ^ col


def on_core(core, action):
    for h in range(2):
        pl.when(core == h)(functools.partial(action, h))


def load(*refs):
    count = len(refs) // 2
    copies = [
        pltpu.make_async_copy(refs[i], refs[count + i], refs[-1].at[i]) for i in range(count)
    ]
    for copy in copies:
        copy.start()
    for copy in copies:
        copy.wait()


def pack(kp, ka, rt, their_i, their_a, my_i, my_a, *packs):
    _, core, _ = place()

    def fill(h):
        for owner, i, a in ((h, my_i, my_a), (1 - h, their_i, their_a)):
            packs[1 - h][owner * kp : (owner + 1) * kp, :] = i[...]
            for half in range(2):
                low = half * kp + owner * ka
                packs[h][low : low + ka, :] = a[:, half * rt : (half + 1) * rt]

    on_core(core, fill)


def prepare(n, kp, rt, *refs):
    direct, swap, energy, packs = refs[: n - 1], refs[n - 1], refs[n], refs[n + 1 : n + 3]
    ladder, scale, lhs, rhs = refs[n + 3 :]
    chip, core, shift = place()

    def gather(h):
        for j in range(n):
            here, moved = pl.ds(j * kp, kp), pl.ds(pl.multiple_of((shift ^ j) * kp, kp), kp)
            if j == 0:
                i, a = packs[1 - h], packs[h]
                i_at, a_at = h * kp, 0
            else:
                mine, gift = (direct[j - 1], 0), (swap, 2 * kp * (j - 1))
                (i, i_at), (a, a_at) = (gift, mine) if h == 0 else (mine, gift)
                i_at += h * kp
            lhs[moved, :] = i[i_at : i_at + kp, :]
            rhs[here, :rt] = a[a_at : a_at + kp, :]
            rhs[here, rt:] = a[a_at + kp : a_at + 2 * kp, :]

    on_core(core, gather)
    row_start = (2 * chip + core) * rt
    col_start = (chip ^ shift) * 2 * rt
    across = energy[:, pl.ds(pl.multiple_of(col_start, 2 * rt), 2 * rt)]
    for i in range(rt // TILE):
        rows = slice(i * TILE, (i + 1) * TILE)
        ladder[rows, :] = lax.dot_general(
            lhs[:, rows], rhs[...], OVER_FIRST, preferred_element_type=jnp.float32
        )
        along = energy[:, pl.ds(pl.multiple_of(row_start + i * TILE, TILE), TILE)]
        down = jnp.broadcast_to(along, (TILE, TILE)).T[:, :1]
        scale[rows, :] = 1.0 / (down + across)


def finish(n, kp, rt, *refs):
    settled, swap, near_i, near_a = refs[: n - 1], refs[n - 1], refs[n], refs[n + 1]
    ladder, scale, out, lhs, rhs, buffer, done = refs[n + 2 :]
    _, core, shift = place()

    def gather(h):
        for j in range(n):
            here, moved = pl.ds(j * kp, kp), pl.ds(pl.multiple_of((shift ^ j) * kp, kp), kp)
            if j == 0:
                (i, i_at), (a, a_at) = (near_i, 0), (near_a, 0)
            else:
                mine, gift = (settled[j - 1], 0), (swap, 2 * kp * (j - 1))
                (i, i_at), (a, a_at) = (gift, mine) if h == 0 else (mine, gift)
            a_at += h * kp
            lhs[here, :] = a[a_at : a_at + kp, :]
            rhs[moved, :rt] = i[i_at : i_at + kp, :]
            rhs[moved, rt:] = i[i_at + kp : i_at + 2 * kp, :]

    on_core(core, gather)
    copies = []
    for i in range(rt // TILE):
        rows = slice(i * TILE, (i + 1) * TILE)
        partner = lax.dot_general(
            lhs[:, rows], rhs[...], OVER_FIRST, preferred_element_type=jnp.float32
        )
        partner = partner.astype(jnp.bfloat16).astype(jnp.float32)
        for part in range(SPLIT):
            size = TILE // SPLIT
            low = i * TILE + part * size
            some = slice(low, low + size)
            rounded = partner[part * size : (part + 1) * size]
            buffer[some, :] = (ladder[some, :] + rounded) * scale[some, :]
            sem = done.at[i * SPLIT + part]
            copies.append(pltpu.make_async_copy(buffer.at[some], out.at[some], sem))
            copies[-1].start()
    for copy in copies:
        copy.wait()


def call(kernel, inputs, placed, out_specs, out_shape, scratch):
    keep = pl.BlockSpec(memory_space=pltpu.VMEM)
    return pl.pallas_call(
        kernel,
        in_specs=[keep] * (len(inputs) + len(placed)),
        out_specs=out_specs,
        out_shape=out_shape,
        scratch_shapes=scratch,
        compiler_params=pltpu.CompilerParams(vmem_limit_bytes=VMEM_LIMIT),
    )(*[pltpu.with_memory_space_constraint(x, pltpu.VMEM) for x in [*inputs, *placed]])


def paired(integrals, amplitudes, energies):
    n = lax.axis_size("col")
    rt, kp = integrals.shape
    ka = amplitudes.shape[0]
    _, core, shift = place()
    first = core == 0

    def send(value, target):
        pairs = [
            ((2 * k + h) * n + c, (2 * tk + th) * n + tc)
            for k in range(n)
            for h in range(2)
            for c in range(n)
            for tk, th, tc in [target(k, h, c)]
        ]
        return lax.ppermute(value, AXES, pairs)

    def other(k, h, c):
        return k, 1 - h, c

    def carrier(j):
        return 1 - j % 2

    their_i, their_a = send(integrals.T, other), send(amplitudes, other)
    keep = pl.BlockSpec(memory_space=pltpu.VMEM)
    mine = (integrals.T, amplitudes)
    mine = pl.pallas_call(
        load,
        in_specs=[pl.BlockSpec(memory_space=pltpu.HBM)] * 2,
        out_specs=[keep] * 2,
        out_shape=[pltpu.VMEM(x.shape, x.dtype) for x in mine],
        scratch_shapes=[pltpu.SemaphoreType.DMA((2,))],
        compiler_params=pltpu.CompilerParams(vmem_limit_bytes=VMEM_LIMIT),
        name="load",
    )(*[pltpu.with_memory_space_constraint(x, pltpu.HBM) for x in mine])
    own = call(
        functools.partial(pack, kp, ka, rt),
        [their_i, their_a],
        mine,
        [keep] * 2,
        [pltpu.VMEM((2 * kp, rt), jnp.bfloat16)] * 2,
        [],
    )
    order = range(n - 1, 0, -1)
    gathered, direct, settled = {0: own[carrier(0)]}, {}, {}
    for j in order:
        gathered[j] = send(
            own[carrier(j)], lambda k, h, c: (k, h, c ^ j) if h == carrier(j) else (k ^ j, h, c)
        )
    for j in order:
        direct[j] = send(
            own[carrier(j)], lambda k, h, c: (k ^ j, 0, c) if h == carrier(j) else (k, 1, c ^ j)
        )
    for j in order:
        settled[j] = send(
            pick(shift ^ j, gathered),
            lambda k, h, c: (k ^ j, 0, c) if h == carrier(k ^ c ^ j) else (k, 1, c ^ j),
        )
    near = pick(shift, gathered)
    far = send(near, other)
    has_a = functools.reduce(
        lambda kept, m: jnp.where(shift == m, core == carrier(m), kept), range(n), first
    )
    near_a, near_i = jnp.where(has_a, near, far), jnp.where(has_a, far, near)
    direct, settled = [[x[j] for j in range(1, n)] for x in (direct, settled)]
    swap_d, swap_s = send(jnp.concatenate(direct), other), send(jnp.concatenate(settled), other)
    early = call(
        functools.partial(prepare, n, kp, rt),
        [*direct, swap_d, energies.reshape(1, -1)],
        own,
        [keep] * 2,
        [pltpu.VMEM((rt, 2 * rt), jnp.float32)] * 2,
        [pltpu.VMEM((n * kp, width), jnp.bfloat16) for width in (rt, 2 * rt)],
    )
    return call(
        functools.partial(finish, n, kp, rt),
        [*settled, swap_s, near_i, near_a],
        early,
        pl.BlockSpec(memory_space=pl.ANY),
        jax.ShapeDtypeStruct((rt, 2 * rt), jnp.float32),
        [
            *[pltpu.VMEM((n * kp, width), jnp.bfloat16) for width in (rt, 2 * rt)],
            pltpu.VMEM((rt, 2 * rt), jnp.float32),
            pltpu.SemaphoreType.DMA((rt // TILE * SPLIT,)),
        ],
    )


def general(integrals, amplitudes, energies):
    rows_tile = integrals.shape[0]
    cols_tile = amplitudes.shape[1]
    n_row = lax.axis_size("row")
    n_col = lax.axis_size("col")
    block = rows_tile // n_col
    panel = lax.all_gather(integrals, "col", axis=1, tiled=True)
    ladder = jnp.dot(
        panel,
        lax.all_gather(amplitudes, "row", axis=0, tiled=True),
        preferred_element_type=jnp.float32,
    )
    rounded = ladder.astype(jnp.bfloat16)
    by_rows = lax.all_to_all(rounded, "col", split_axis=0, concat_axis=1, tiled=True)
    lifted = lax.all_to_all(by_rows, "row", split_axis=1, concat_axis=0, tiled=True)
    shaped = lifted.reshape(n_row, 1, block, n_col * block)
    settled = lax.all_to_all(shaped, "col", split_axis=0, concat_axis=1, tiled=True)
    partner = settled.reshape(n_row * block, n_col * block).T.astype(jnp.float32)
    row_start = lax.axis_index("row") * rows_tile
    col_start = lax.axis_index("col") * cols_tile
    row_energy = lax.dynamic_slice_in_dim(energies, row_start, rows_tile, 0)
    col_energy = lax.dynamic_slice_in_dim(energies, col_start, cols_tile, 0)
    return (ladder + partner) / (row_energy[:, None] + col_energy[None, :])


def body(integrals, amplitudes, energies):
    rt, kp = integrals.shape
    n_row, n_col = lax.axis_size("row"), lax.axis_size("col")
    fits = (
        n_row == 2 * n_col
        and n_col & (n_col - 1) == 0
        and amplitudes.shape == (kp // 2, 2 * rt)
        and rt % 128 == 0
        and kp % 16 == 0
    )
    return (paired if fits else general)(integrals, amplitudes, energies)


def solution(mesh):
    placed = (P("row", "col"), P("row", "col"), P())
    return jax.shard_map(
        body, mesh=mesh, in_specs=placed, out_specs=P("row", "col"), check_vma=False
    )
```

```python
import functools

import jax
import jax.numpy as jnp
from jax import lax
from jax.experimental import pallas as pl
from jax.experimental.pallas import tpu as pltpu
from jax.sharding import PartitionSpec as P


AXES = ("row", "col")
TILE = 128
SPLIT = 2
VMEM_LIMIT = 12 * 2**20
OVER_FIRST = (((0,), (0,)), ((), ()))


def pick(index, pieces):
    return functools.reduce(
        lambda kept, i: jnp.where(index == i, pieces[i], kept),
        range(1, len(pieces)),
        pieces[0],
    )


def place():
    row, col = lax.axis_index("row"), lax.axis_index("col")
    return row // 2, row % 2, (row // 2) ^ col


def on_core(core, action):
    for h in range(2):
        pl.when(core == h)(functools.partial(action, h))


def load(*refs):
    count = len(refs) // 2
    copies = [
        pltpu.make_async_copy(refs[i], refs[count + i], refs[-1].at[i]) for i in range(count)
    ]
    for copy in copies:
        copy.start()
    for copy in copies:
        copy.wait()


def pack(kp, ka, rt, their_i, their_a, my_i, my_a, *packs):
    _, core, _ = place()

    def fill(h):
        for owner, i, a in ((h, my_i, my_a), (1 - h, their_i, their_a)):
            packs[1 - h][owner * kp : (owner + 1) * kp, :] = i[...]
            for half in range(2):
                low = half * kp + owner * ka
                packs[h][low : low + ka, :] = a[:, half * rt : (half + 1) * rt]

    on_core(core, fill)


def prepare(n, kp, rt, *refs):
    direct, swap, energy, packs = refs[: n - 1], refs[n - 1], refs[n], refs[n + 1 : n + 3]
    ladder, scale, lhs, rhs = refs[n + 3 :]
    chip, core, shift = place()

    def gather(h):
        for j in range(n):
            here, moved = pl.ds(j * kp, kp), pl.ds(pl.multiple_of((shift ^ j) * kp, kp), kp)
            if j == 0:
                i, a = packs[1 - h], packs[h]
                i_at, a_at = h * kp, 0
            else:
                mine, gift = (direct[j - 1], 0), (swap, 2 * kp * (j - 1))
                (i, i_at), (a, a_at) = (gift, mine) if h == 0 else (mine, gift)
                i_at += h * kp
            lhs[moved, :] = i[i_at : i_at + kp, :]
            rhs[here, :rt] = a[a_at : a_at + kp, :]
            rhs[here, rt:] = a[a_at + kp : a_at + 2 * kp, :]

    on_core(core, gather)
    row_start = (2 * chip + core) * rt
    col_start = (chip ^ shift) * 2 * rt
    across = energy[:, pl.ds(pl.multiple_of(col_start, 2 * rt), 2 * rt)]
    for i in range(rt // TILE):
        rows = slice(i * TILE, (i + 1) * TILE)
        ladder[rows, :] = lax.dot_general(
            lhs[:, rows], rhs[...], OVER_FIRST, preferred_element_type=jnp.float32
        )
        along = energy[:, pl.ds(pl.multiple_of(row_start + i * TILE, TILE), TILE)]
        down = jnp.broadcast_to(along, (TILE, TILE)).T[:, :1]
        scale[rows, :] = 1.0 / (down + across)


def finish(n, kp, rt, *refs):
    settled, swap, near_i, near_a = refs[: n - 1], refs[n - 1 : n + 1], refs[n + 1], refs[n + 2]
    ladder, scale, out, lhs, rhs, buffer, done = refs[n + 3 :]
    _, core, shift = place()

    def gather(h):
        for j in range(n):
            here, moved = pl.ds(j * kp, kp), pl.ds(pl.multiple_of((shift ^ j) * kp, kp), kp)
            if j == 0:
                (i, i_at), (a, a_at) = (near_i, 0), (near_a, 0)
            else:
                mine = (settled[j - 1], 0)
                gift = (swap[0], 0) if j == 1 else (swap[1], 2 * kp * (j - 2))
                (i, i_at), (a, a_at) = (gift, mine) if h == 0 else (mine, gift)
            a_at += h * kp
            lhs[here, :] = a[a_at : a_at + kp, :]
            rhs[moved, :rt] = i[i_at : i_at + kp, :]
            rhs[moved, rt:] = i[i_at + kp : i_at + 2 * kp, :]

    on_core(core, gather)
    copies = []
    for i in range(rt // TILE):
        rows = slice(i * TILE, (i + 1) * TILE)
        partner = lax.dot_general(
            lhs[:, rows], rhs[...], OVER_FIRST, preferred_element_type=jnp.float32
        )
        partner = partner.astype(jnp.bfloat16).astype(jnp.float32)
        for part in range(SPLIT):
            size = TILE // SPLIT
            low = i * TILE + part * size
            some = slice(low, low + size)
            rounded = partner[part * size : (part + 1) * size]
            buffer[some, :] = (ladder[some, :] + rounded) * scale[some, :]
            sem = done.at[i * SPLIT + part]
            copies.append(pltpu.make_async_copy(buffer.at[some], out.at[some], sem))
            copies[-1].start()
    for copy in copies:
        copy.wait()


def call(kernel, inputs, placed, out_specs, out_shape, scratch):
    keep = pl.BlockSpec(memory_space=pltpu.VMEM)
    return pl.pallas_call(
        kernel,
        in_specs=[keep] * (len(inputs) + len(placed)),
        out_specs=out_specs,
        out_shape=out_shape,
        scratch_shapes=scratch,
        compiler_params=pltpu.CompilerParams(vmem_limit_bytes=VMEM_LIMIT),
    )(*[pltpu.with_memory_space_constraint(x, pltpu.VMEM) for x in [*inputs, *placed]])


def paired(integrals, amplitudes, energies):
    n = lax.axis_size("col")
    rt, kp = integrals.shape
    ka = amplitudes.shape[0]
    _, core, shift = place()
    first = core == 0

    def send(value, target):
        pairs = [
            ((2 * k + h) * n + c, (2 * tk + th) * n + tc)
            for k in range(n)
            for h in range(2)
            for c in range(n)
            for tk, th, tc in [target(k, h, c)]
        ]
        return lax.ppermute(value, AXES, pairs)

    def other(k, h, c):
        return k, 1 - h, c

    def carrier(j):
        return 1 - j % 2

    their_i, their_a = send(integrals.T, other), send(amplitudes, other)
    keep = pl.BlockSpec(memory_space=pltpu.VMEM)
    mine = (integrals.T, amplitudes)
    mine = pl.pallas_call(
        load,
        in_specs=[pl.BlockSpec(memory_space=pltpu.HBM)] * 2,
        out_specs=[keep] * 2,
        out_shape=[pltpu.VMEM(x.shape, x.dtype) for x in mine],
        scratch_shapes=[pltpu.SemaphoreType.DMA((2,))],
        compiler_params=pltpu.CompilerParams(vmem_limit_bytes=VMEM_LIMIT),
        name="load",
    )(*[pltpu.with_memory_space_constraint(x, pltpu.HBM) for x in mine])
    own = call(
        functools.partial(pack, kp, ka, rt),
        [their_i, their_a],
        mine,
        [keep] * 2,
        [pltpu.VMEM((2 * kp, rt), jnp.bfloat16)] * 2,
        [],
    )
    order = range(n - 1, 0, -1)
    gathered, direct, settled = {0: own[carrier(0)]}, {}, {}
    for j in order:
        gathered[j] = send(
            own[carrier(j)], lambda k, h, c: (k, h, c ^ j) if h == carrier(j) else (k ^ j, h, c)
        )
    for j in order:
        direct[j] = send(
            own[carrier(j)], lambda k, h, c: (k ^ j, 0, c) if h == carrier(j) else (k, 1, c ^ j)
        )
    for j in order:
        settled[j] = send(
            pick(shift ^ j, gathered),
            lambda k, h, c: (k ^ j, 0, c) if h == carrier(k ^ c ^ j) else (k, 1, c ^ j),
        )
    near = pick(shift, gathered)
    swap_g = send(jnp.concatenate([*[direct[j] for j in range(1, n)], near]), other)
    far, swap_d = swap_g[2 * kp * (n - 1) :], swap_g[: 2 * kp * (n - 1)]
    has_a = functools.reduce(
        lambda kept, m: jnp.where(shift == m, core == carrier(m), kept), range(n), first
    )
    near_a, near_i = jnp.where(has_a, near, far), jnp.where(has_a, far, near)
    direct, settled = [[x[j] for j in range(1, n)] for x in (direct, settled)]
    swap_s = [send(settled[0], other), send(jnp.concatenate(settled[1:]), other)]
    early = call(
        functools.partial(prepare, n, kp, rt),
        [*direct, swap_d, energies.reshape(1, -1)],
        own,
        [keep] * 2,
        [pltpu.VMEM((rt, 2 * rt), jnp.float32)] * 2,
        [pltpu.VMEM((n * kp, width), jnp.bfloat16) for width in (rt, 2 * rt)],
    )
    return call(
        functools.partial(finish, n, kp, rt),
        [*settled, *swap_s, near_i, near_a],
        early,
        pl.BlockSpec(memory_space=pl.ANY),
        jax.ShapeDtypeStruct((rt, 2 * rt), jnp.float32),
        [
            *[pltpu.VMEM((n * kp, width), jnp.bfloat16) for width in (rt, 2 * rt)],
            pltpu.VMEM((rt, 2 * rt), jnp.float32),
            pltpu.SemaphoreType.DMA((rt // TILE * SPLIT,)),
        ],
    )


def general(integrals, amplitudes, energies):
    rows_tile = integrals.shape[0]
    cols_tile = amplitudes.shape[1]
    n_row = lax.axis_size("row")
    n_col = lax.axis_size("col")
    block = rows_tile // n_col
    panel = lax.all_gather(integrals, "col", axis=1, tiled=True)
    ladder = jnp.dot(
        panel,
        lax.all_gather(amplitudes, "row", axis=0, tiled=True),
        preferred_element_type=jnp.float32,
    )
    rounded = ladder.astype(jnp.bfloat16)
    by_rows = lax.all_to_all(rounded, "col", split_axis=0, concat_axis=1, tiled=True)
    lifted = lax.all_to_all(by_rows, "row", split_axis=1, concat_axis=0, tiled=True)
    shaped = lifted.reshape(n_row, 1, block, n_col * block)
    settled = lax.all_to_all(shaped, "col", split_axis=0, concat_axis=1, tiled=True)
    partner = settled.reshape(n_row * block, n_col * block).T.astype(jnp.float32)
    row_start = lax.axis_index("row") * rows_tile
    col_start = lax.axis_index("col") * cols_tile
    row_energy = lax.dynamic_slice_in_dim(energies, row_start, rows_tile, 0)
    col_energy = lax.dynamic_slice_in_dim(energies, col_start, cols_tile, 0)
    return (ladder + partner) / (row_energy[:, None] + col_energy[None, :])


def body(integrals, amplitudes, energies):
    rt, kp = integrals.shape
    n_row, n_col = lax.axis_size("row"), lax.axis_size("col")
    fits = (
        n_row == 2 * n_col
        and n_col & (n_col - 1) == 0
        and amplitudes.shape == (kp // 2, 2 * rt)
        and rt % 128 == 0
        and kp % 16 == 0
    )
    return (paired if fits else general)(integrals, amplitudes, energies)


def solution(mesh):
    placed = (P("row", "col"), P("row", "col"), P())
    return jax.shard_map(
        body, mesh=mesh, in_specs=placed, out_specs=P("row", "col"), check_vma=False
    )
```
